32 devices in a mesh: mp: 8 (over z, x), dp: 4 (over y, core).
Axes of the slice: x: 2, y: 2, z: 4, core: 2. Of those that a mesh axis runs over, the one named last changes fastest.
Arguments:
- inputs: bfloat16 [768, 8192], P('dp', 'mp'), may hold values from -42 to 42
- out_grads: bfloat16 [768, 16384], P('dp', 'mp'), may hold values from -42 to 42
- weight: bfloat16 [8192, 16384], P('dp', 'mp'), may hold values from -0.25 to 0.25
- enc_in: bfloat16 [8192, 1920], P('mp'), may hold values from -0.0625 to 0.0625
- dec_in: bfloat16 [1920, 8192], P(None, 'mp'), may hold values from -0.125 to 0.125
- enc_out: bfloat16 [16384, 1920], P('mp'), may hold values from -0.046875 to 0.046875
- dec_out: bfloat16 [1920, 16384], P(None, 'mp'), may hold values from -0.125 to 0.125
Outputs:
- post_out: bfloat16 [768, 16384], P('dp', 'mp')
- grad_in: bfloat16 [768, 8192], P('dp', 'mp')
The draws below stay inside these ranges and needn't reach their ends.
All inputs are finite; a program needn't handle non-finite values.
Results may differ from the reference program's by a relative error of at most 0.024.
Values may be sent and summed in bfloat16 or wider, within the bound.
No kernel may reach another device: no remote copies, remote signals or barrier semaphores. Data moves between devices by JAX's collectives and lax.ppermute only.
A program may use at most 128 MiB of HBM per device.

```python
import jax
import jax.numpy as jnp
from jax import lax

D = 8192
FW = 16384
R = 1920
TOKENS = 768
N_MP = 8


def ramped(key, rows, cols):
    key_vals = jax.random.fold_in(key, 11)
    column_ramp = 1.0 + 2.0 * jnp.arange(cols, dtype=jnp.float32)[None, :] / cols
    values = jax.random.truncated_normal(key_vals, -4.0, 4.0, (rows, cols), jnp.float32)
    result = values * column_ramp
    return result


def draw_inputs(key, part):
    return ramped(jax.random.fold_in(key, 1), TOKENS, D).astype(jnp.bfloat16)


def draw_out_grads(key, part):
    return ramped(jax.random.fold_in(key, 2), TOKENS, FW).astype(jnp.bfloat16)


def block_levels(own_key, dims, shards, least, high):
    factor_of, own = 1.0, jax.random.fold_in(own_key, 6)
    for dim, blocks in shards:
        heights = jnp.exp(jax.random.uniform(jax.random.fold_in(own, dim), (blocks,), jnp.float32, least / len(shards), high / len(shards)))
        factor_of = factor_of * jnp.repeat(heights, dims[dim] // blocks).reshape([-1 if axis == dim else 1 for axis in range(len(dims))])
    return factor_of


def noise(stream_key, extent, spread, limit, split=(), kind=jnp.bfloat16):
    values = spread * jax.random.normal(stream_key, extent, jnp.float32)
    if split:
        values = values * block_levels(stream_key, extent, split, -0.22, 0.18)
    return jnp.clip(values, -limit, limit).astype(kind)


def setup_inputs(seed: int = 0) -> dict:
    arg_keys = jax.random.split(jax.random.key(seed), 8)
    inputs = draw_inputs(jax.random.fold_in(arg_keys[7], 71), 0)
    out_grads = draw_out_grads(jax.random.fold_in(arg_keys[7], 71), 0)
    weight = noise(arg_keys[2], (D, FW), (D // 16) ** -0.5, 0.25, ((0, 4), (1, 8)))
    enc_in = noise(arg_keys[3], (D, R), D ** -0.5, 0.0625, ((0, 8),))
    dec_in = noise(arg_keys[4], (R, D), R ** -0.5, 0.125, ((1, 8),))
    enc_out = noise(arg_keys[5], (FW, R), FW ** -0.5, 0.046875, ((0, 8),))
    dec_out = noise(arg_keys[6], (R, FW), R ** -0.5, 0.125, ((1, 8),))
    return dict(inputs=inputs, out_grads=out_grads, weight=weight, enc_in=enc_in, dec_in=dec_in, enc_out=enc_out, dec_out=dec_out)


epsilon = 1e-06
step_size = 0.25

def silu_slope(value):
    sig = jax.nn.sigmoid(value)
    return sig * (1.0 + value * (1.0 - sig))

def reference(inputs, out_grads, weight, enc_in, dec_in, enc_out, dec_out):
    factor = step_size / D
    input_wide = inputs.astype(jnp.float32)
    grad_wide = out_grads.astype(jnp.float32)
    input_scale = lax.rsqrt(lax.optimization_barrier(jnp.sum(input_wide * input_wide, axis=1, keepdims=True)) / D + epsilon)
    grad_scale = lax.rsqrt(lax.optimization_barrier(jnp.sum(grad_wide * grad_wide, axis=1, keepdims=True)) / FW + epsilon)
    input_hidden = jax.nn.relu(jnp.dot(inputs, enc_in, preferred_element_type=jnp.float32) * input_scale).astype(jnp.bfloat16)
    grad_hidden = jax.nn.relu(jnp.dot(out_grads, enc_out, preferred_element_type=jnp.float32) * grad_scale).astype(jnp.bfloat16)
    edited_in = (input_wide + jnp.dot(input_hidden, dec_in, preferred_element_type=jnp.float32)).astype(jnp.bfloat16)
    edited_grad = (grad_wide + jnp.dot(grad_hidden, dec_out, preferred_element_type=jnp.float32)).astype(jnp.bfloat16)
    kernel = (jnp.dot(inputs, edited_in.T, preferred_element_type=jnp.float32) * factor).astype(jnp.bfloat16)
    post_full = jnp.dot(inputs, weight, preferred_element_type=jnp.float32) - jnp.dot(kernel, edited_grad, preferred_element_type=jnp.float32)
    post_out = post_full.astype(jnp.bfloat16)
    cotangent = (grad_wide * silu_slope(post_full)).astype(jnp.bfloat16)
    width = FW // N_MP
    weight_blocks = weight.reshape(D, N_MP, width).transpose(1, 0, 2)
    cot_blocks = cotangent.reshape(TOKENS, N_MP, width).transpose(1, 0, 2)

    def add_block(total, pair):
        cot_piece, weight_piece = pair
        part = jnp.dot(cot_piece, weight_piece.T, preferred_element_type=jnp.float32).astype(jnp.bfloat16)
        part = lax.optimization_barrier(part)
        return (total + part.astype(jnp.float32), None)
    back, _ = lax.scan(add_block, jnp.zeros((TOKENS, D), jnp.float32), (cot_blocks, weight_blocks))
    back_kernel = (jnp.dot(cotangent, edited_grad.T, preferred_element_type=jnp.float32) * factor).astype(jnp.bfloat16)
    grad_in = (back - jnp.dot(back_kernel, edited_in, preferred_element_type=jnp.float32)).astype(jnp.bfloat16)
    return (post_out, grad_in)
```

```python
import jax
import jax.numpy as jnp
from jax import lax
from jax.sharding import PartitionSpec as P


epsilon = 1e-06
step_size = 0.25
bf16 = jnp.bfloat16
f32 = jnp.float32


def silu_slope(value):
    sig = jax.nn.sigmoid(value)
    return sig * (1.0 + value * (1.0 - sig))


def dot(a, b):
    return jnp.dot(a, b, preferred_element_type=f32)


def dot_t(a, b):
    return lax.dot_general(a, b, (((a.ndim - 1,), (1,)), ((), ())), preferred_element_type=f32)


class Grid:
    def __init__(self, mp, dp):
        self.mp, self.dp = mp, dp
        self.nz, self.nx, self.ny = dp, mp // dp, dp // 2
        self.xbits = [1 << b for b in range(self.nx.bit_length() - 1)]
        self.zbits = [1 << b for b in range(self.nz.bit_length() - 1)]

    def place(self):
        m, d = lax.axis_index("mp"), lax.axis_index("dp")
        self.z, self.x = m // self.nx, m % self.nx
        self.d = d

    def swap(self, a, z=0, x=0, d=0):
        perm = []
        for zz in range(self.nz):
            for xx in range(self.nx):
                for dd in range(self.dp):
                    src = (zz * self.nx + xx) * self.dp + dd
                    dst = ((zz ^ z) * self.nx + (xx ^ x)) * self.dp + (dd ^ d)
                    perm.append((src, dst))
        return lax.ppermute(a, ("mp", "dp"), perm)


def halves(a, flag, axis):
    h = a.shape[axis] // 2
    kept = lax.dynamic_slice_in_dim(a, flag * h, h, axis)
    sent = lax.dynamic_slice_in_dim(a, (1 - flag) * h, h, axis)
    return kept, sent


def joined(own, got, flag, axis):
    first = jnp.where(flag == 0, own, got)
    second = jnp.where(flag == 0, got, own)
    return jnp.concatenate([first, second], axis=axis)


def bit(value, b):
    return (value // b) % 2


def shards(grid, inputs, out_grads, weight, enc_in, dec_in, enc_out, dec_out):
    g = grid
    g.place()
    nx, ny = g.nx, g.ny
    tok, fb = inputs.shape
    cols = out_grads.shape[1]
    features = fb * g.mp
    hidden = cols * g.mp
    factor = step_size / features

    xsteps = [(dict(x=b), bit(g.x, b)) for b in g.xbits]
    zsteps = [(dict(z=b), bit(g.z, b)) for b in g.zbits]

    def scatter_rows(a):
        for where, flag in xsteps + zsteps:
            kept, sent = halves(a, flag, 0)
            a = kept + g.swap(sent.astype(bf16), **where).astype(f32)
        return a

    def gather_rows(a):
        for where, flag in reversed(xsteps + zsteps):
            a = joined(a, g.swap(a, **where), flag, 0)
        return a

    def editor(rows, enc, dec, width):
        wide = rows.astype(f32)
        squares = jnp.sum((wide * wide).reshape(tok, -1, 128), axis=1)
        message = jnp.concatenate([dot(rows, enc), squares], axis=1)
        message = scatter_rows(message)
        r = enc.shape[1]
        total = jnp.sum(message[:, r:], axis=1, keepdims=True)
        act = jax.nn.relu(message[:, :r] * lax.rsqrt(total / width + epsilon)).astype(bf16)
        act = gather_rows(act)
        return (wide + dot(act, dec)).astype(bf16)

    def over_dp(a):
        parts = [a] + [g.swap(a, d=2 * s) for s in range(1, ny)]
        stack = jnp.concatenate(parts, axis=0)
        other = g.swap(stack, d=1)
        return jnp.concatenate([stack, other], axis=0)

    def sum_mp(a):
        for where, flag in xsteps:
            kept, sent = halves(a, flag, 0)
            a = kept + g.swap(sent.astype(bf16), **where).astype(f32)
        for where, _ in zsteps:
            a = a + g.swap(a.astype(bf16), **where).astype(f32)
        a = (a * factor).astype(bf16)
        for where, flag in reversed(xsteps):
            a = joined(a, g.swap(a, **where), flag, 0)
        return a

    weights = [weight, g.swap(weight, d=1)]

    edited_in = editor(inputs, enc_in, dec_in, features)
    edited_grad = editor(out_grads, enc_out, dec_out, hidden)

    block = inputs[None]
    for b in reversed(g.zbits):
        flag = bit(g.z, b) ^ bit(g.d, b)
        block = joined(block, g.swap(block, z=b), flag, 0)
    nb = len(g.zbits)
    block = block.reshape((2,) * nb + (tok, fb))
    block = block.transpose(tuple(reversed(range(nb))) + (nb, nb + 1))
    block = block.reshape(ny, 2, tok, fb)
    parts = [block[0]] + [g.swap(block[s], d=2 * s) for s in range(1, ny)]
    block = jnp.stack(parts)
    for where, flag in reversed(xsteps):
        block = joined(block, g.swap(block, **where), flag, 3)
    block = block.reshape((ny, 2, tok) + (2,) * len(xsteps) + (fb,))
    n3 = 3 + len(xsteps)
    block = block.transpose((0, 1, 2) + tuple(reversed(range(3, n3))) + (n3,))
    block = block.reshape(ny, 2, tok, nx * fb)

    rows0 = block[:, 0].reshape(ny * tok, nx * fb)
    rows1 = block[:, 1].reshape(ny * tok, nx * fb)
    base = (dot(rows0, weights[0]) + dot(rows1, weights[1])).reshape(ny, tok, cols)

    edits_all = over_dp(edited_in)
    grads_all = over_dp(edited_grad)
    kernel = sum_mp(dot_t(inputs, edits_all))
    post_full = base[0] - dot(kernel, grads_all)
    for s in range(1, ny):
        post_full = post_full + g.swap(base[s].astype(bf16), d=2 * s).astype(f32)
    cotangent = (out_grads.astype(f32) * silu_slope(post_full)).astype(bf16)

    back_kernel = sum_mp(dot_t(cotangent, grads_all))
    cots = jnp.concatenate([cotangent] + [g.swap(cotangent, d=2 * s) for s in range(1, ny)], axis=0)
    back = jnp.stack([dot_t(cots, w).reshape(ny, tok, nx * fb) for w in weights], axis=1)
    back = back.reshape((ny, 2, tok) + (2,) * len(xsteps) + (fb,))
    for i, (where, flag) in enumerate(xsteps):
        axis = 3 + len(xsteps) - 1 - i
        kept, sent = halves(back, flag, axis)
        back = kept + g.swap(sent.astype(bf16), **where).astype(f32)
    back = back.reshape(ny, 2, tok, fb)
    mine = [back[0]] + [g.swap(back[s].astype(bf16), d=2 * s).astype(f32) for s in range(1, ny)]
    back = jnp.stack(mine).reshape((2,) * nb + (tok, fb))
    for i, b in enumerate(g.zbits):
        kept, sent = halves(back, bit(g.z, b) ^ bit(g.d, b), nb - 1 - i)
        back = kept + g.swap(sent.astype(bf16), z=b).astype(f32)
    back = back.reshape(tok, fb)
    grad_in = (back - dot(back_kernel, edits_all)).astype(bf16)
    return (post_full.astype(bf16), grad_in)


def solution(mesh):
    grid = Grid(mesh.shape["mp"], mesh.shape["dp"])

    def body(*args):
        return shards(grid, *args)

    in_specs = (
        P("dp", "mp"),
        P("dp", "mp"),
        P("dp", "mp"),
        P("mp", None),
        P(None, "mp"),
        P("mp", None),
        P(None, "mp"),
    )
    out_specs = (P("dp", "mp"), P("dp", "mp"))
    return jax.shard_map(body, mesh=mesh, in_specs=in_specs, out_specs=out_specs, check_vma=False)
```

```python
import jax
import jax.numpy as jnp
from jax import lax
from jax.sharding import PartitionSpec as P


epsilon = 1e-06
step_size = 0.25
bf16 = jnp.bfloat16
f32 = jnp.float32


def silu_slope(value):
    sig = jax.nn.sigmoid(value)
    return sig * (1.0 + value * (1.0 - sig))


def dot(a, b):
    return jnp.dot(a, b, preferred_element_type=f32)


def dot_t(a, b):
    return lax.dot_general(a, b, (((a.ndim - 1,), (1,)), ((), ())), preferred_element_type=f32)


class Grid:
    def __init__(self, mp, dp):
        self.mp, self.dp = mp, dp
        self.nz, self.nx, self.ny = dp, mp // dp, dp // 2
        self.xbits = [1 << b for b in range(self.nx.bit_length() - 1)]
        self.zbits = [1 << b for b in range(self.nz.bit_length() - 1)]

    def place(self):
        m, d = lax.axis_index("mp"), lax.axis_index("dp")
        self.z, self.x = m // self.nx, m % self.nx
        self.d = d

    def swap(self, a, z=0, x=0, d=0):
        perm = []
        for zz in range(self.nz):
            for xx in range(self.nx):
                for dd in range(self.dp):
                    src = (zz * self.nx + xx) * self.dp + dd
                    dst = ((zz ^ z) * self.nx + (xx ^ x)) * self.dp + (dd ^ d)
                    perm.append((src, dst))
        return lax.ppermute(a, ("mp", "dp"), perm)


def halves(a, flag, axis):
    h = a.shape[axis] // 2
    kept = lax.dynamic_slice_in_dim(a, flag * h, h, axis)
    sent = lax.dynamic_slice_in_dim(a, (1 - flag) * h, h, axis)
    return kept, sent


def joined(own, got, flag, axis):
    first = jnp.where(flag == 0, own, got)
    second = jnp.where(flag == 0, got, own)
    return jnp.concatenate([first, second], axis=axis)


def bit(value, b):
    return (value // b) % 2


def shards(grid, inputs, out_grads, weight, enc_in, dec_in, enc_out, dec_out):
    g = grid
    g.place()
    nx, ny = g.nx, g.ny
    tok, fb = inputs.shape
    cols = out_grads.shape[1]
    features = fb * g.mp
    hidden = cols * g.mp
    factor = step_size / features

    xsteps = [(dict(x=b), bit(g.x, b)) for b in g.xbits]
    zsteps = [(dict(z=b), bit(g.z, b)) for b in g.zbits]

    def scatter_rows(a):
        for where, flag in xsteps + zsteps:
            kept, sent = halves(a, flag, 0)
            a = kept + g.swap(sent.astype(bf16), **where).astype(f32)
        return a

    def gather_rows(a):
        for where, flag in reversed(xsteps + zsteps):
            a = joined(a, g.swap(a, **where), flag, 0)
        return a

    def editor(rows, enc, dec, width):
        wide = rows.astype(f32)
        squares = jnp.sum((wide * wide).reshape(tok, -1, 128), axis=1)
        message = jnp.concatenate([dot(rows, enc), squares], axis=1)
        message = scatter_rows(message)
        r = enc.shape[1]
        total = jnp.sum(message[:, r:], axis=1, keepdims=True)
        act = jax.nn.relu(message[:, :r] * lax.rsqrt(total / width + epsilon)).astype(bf16)
        act = gather_rows(act)
        return (wide + dot(act, dec)).astype(bf16)

    def over_dp(a):
        parts = [a] + [g.swap(a, d=2 * s) for s in range(1, ny)]
        stack = jnp.concatenate(parts, axis=0)
        other = g.swap(stack, d=1)
        return jnp.concatenate([stack, other], axis=0)

    def sum_mp(a):
        for where, flag in xsteps:
            kept, sent = halves(a, flag, 0)
            a = kept + g.swap(sent.astype(bf16), **where).astype(f32)
        for where, _ in zsteps:
            a = a + g.swap(a.astype(bf16), **where).astype(f32)
        a = (a * factor).astype(bf16)
        for where, flag in reversed(xsteps):
            a = joined(a, g.swap(a, **where), flag, 0)
        return a

    with jax.named_scope("sibling"):
        weights = [weight, g.swap(weight, d=1)]

    with jax.named_scope("edit_in"):
        edited_in = editor(inputs, enc_in, dec_in, features)
    with jax.named_scope("edit_grad"):
        edited_grad = editor(out_grads, enc_out, dec_out, hidden)

    block = inputs[None]
    for b in reversed(g.zbits):
        flag = bit(g.z, b) ^ bit(g.d, b)
        with jax.named_scope(f"rows_z_{b}"):
            block = joined(block, g.swap(block, z=b), flag, 0)
    nb = len(g.zbits)
    block = block.reshape((2,) * nb + (tok, fb))
    block = block.transpose(tuple(reversed(range(nb))) + (nb, nb + 1))
    block = block.reshape(ny, 2, tok, fb)

    def base_of(part, name):
        with jax.named_scope(name):
            for where, flag in reversed(xsteps):
                part = joined(part, g.swap(part, **where), flag, 2)
            part = part.reshape((2, tok) + (2,) * len(xsteps) + (fb,))
            n2 = 2 + len(xsteps)
            part = part.transpose((0, 1) + tuple(reversed(range(2, n2))) + (n2,)).reshape(2, tok, nx * fb)
            return dot(part[0], weights[0]) + dot(part[1], weights[1])

    far = []
    for s in range(1, ny):
        with jax.named_scope(f"rows_y_{s}"):
            part = g.swap(block[s], d=2 * s)
        part = base_of(part, f"rows_far_{s}")
        with jax.named_scope(f"base_y_{s}"):
            far.append(g.swap(part.astype(bf16), d=2 * s).astype(f32))
    base = base_of(block[0], "rows_own")

    with jax.named_scope("edits_all"):
        edits_all = over_dp(edited_in)
    with jax.named_scope("grads_all"):
        grads_all = over_dp(edited_grad)
    with jax.named_scope("kernel"):
        kernel = sum_mp(dot_t(inputs, edits_all))
    post_full = base - dot(kernel, grads_all)
    for part in far:
        post_full = post_full + part
    cotangent = (out_grads.astype(f32) * silu_slope(post_full)).astype(bf16)

    chunk = tok // 2

    def weight_rows(k, x):
        return lax.dynamic_slice_in_dim(weights[k], x * fb, fb, 0)

    def over_x(cot, name):
        with jax.named_scope(name):
            total = [None, None]
            for t in range(1, nx):
                sent = jnp.stack([dot_t(cot, weight_rows(k, g.x ^ t)).astype(bf16) for k in range(2)])
                got = g.swap(sent, x=t)
                for k in range(2):
                    total[k] = got[k].astype(f32) if total[k] is None else total[k] + got[k].astype(f32)
            for k in range(2):
                own = dot_t(cot, weight_rows(k, g.x))
                total[k] = own if total[k] is None else own + total[k]
            return total

    def over_z0(pair, name):
        with jax.named_scope(name):
            flag = bit(g.z, 1) ^ bit(g.d, 1)
            kept = jnp.where(flag == 0, pair[0], pair[1])
            sent = jnp.where(flag == 0, pair[1], pair[0]).astype(bf16)
            return kept + g.swap(sent, z=1).astype(f32)

    others = {}
    for h in range(2):
        for s in range(1, ny):
            with jax.named_scope(f"cot_{s}_{h}"):
                others[s, h] = g.swap(cotangent[h * chunk : (h + 1) * chunk], d=2 * s)
    with jax.named_scope("back_kernel"):
        back_kernel = sum_mp(dot_t(cotangent, grads_all))
        correction = dot(back_kernel, edits_all)
    own = over_z0(over_x(cotangent, "own_x"), "own_z")
    out = []
    for h in range(2):
        blocks = [own[h * chunk : (h + 1) * chunk]]
        for s in range(1, ny):
            pair = over_x(others[s, h], f"far_x_{s}_{h}")
            with jax.named_scope(f"far_y_{s}_{h}"):
                pair = g.swap(jnp.stack(pair).astype(bf16), d=2 * s).astype(f32)
            blocks.append(over_z0(pair, f"far_z_{s}_{h}"))
        for b in g.zbits[1:]:
            flag = bit(g.z, b) ^ bit(g.d, b)
            with jax.named_scope(f"last_{b}_{h}"):
                kept = [jnp.where(flag == 0, p, q) for p, q in zip(blocks[::2], blocks[1::2])]
                sent = [jnp.where(flag == 0, q, p).astype(bf16) for p, q in zip(blocks[::2], blocks[1::2])]
                blocks = [p + g.swap(q, z=b).astype(f32) for p, q in zip(kept, sent)]
        out.append((blocks[0] - correction[h * chunk : (h + 1) * chunk]).astype(bf16))
    grad_in = jnp.concatenate(out, axis=0)
    return (post_full.astype(bf16), grad_in)


def solution(mesh):
    grid = Grid(mesh.shape["mp"], mesh.shape["dp"])

    def body(*args):
        return shards(grid, *args)

    in_specs = (
        P("dp", "mp"),
        P("dp", "mp"),
        P("dp", "mp"),
        P("mp", None),
        P(None, "mp"),
        P("mp", None),
        P(None, "mp"),
    )
    out_specs = (P("dp", "mp"), P("dp", "mp"))
    return jax.shard_map(body, mesh=mesh, in_specs=in_specs, out_specs=out_specs, check_vma=False)
```

```python
import jax
import jax.numpy as jnp
from jax import lax
from jax.sharding import PartitionSpec as P


epsilon = 1e-06
step_size = 0.25
bf16 = jnp.bfloat16
f32 = jnp.float32


def silu_slope(value):
    sig = jax.nn.sigmoid(value)
    return sig * (1.0 + value * (1.0 - sig))


def dot(a, b):
    return jnp.dot(a, b, preferred_element_type=f32)


def dot_t(a, b):
    return lax.dot_general(a, b, (((a.ndim - 1,), (1,)), ((), ())), preferred_element_type=f32)


class Grid:
    def __init__(self, mp, dp):
        self.mp, self.dp = mp, dp
        self.nz, self.nx, self.ny = dp, mp // dp, dp // 2
        self.xbits = [1 << b for b in range(self.nx.bit_length() - 1)]
        self.zbits = [1 << b for b in range(self.nz.bit_length() - 1)]

    def place(self):
        m, d = lax.axis_index("mp"), lax.axis_index("dp")
        self.z, self.x = m // self.nx, m % self.nx
        self.d = d

    def swap(self, a, z=0, x=0, d=0):
        perm = []
        for zz in range(self.nz):
            for xx in range(self.nx):
                for dd in range(self.dp):
                    src = (zz * self.nx + xx) * self.dp + dd
                    dst = ((zz ^ z) * self.nx + (xx ^ x)) * self.dp + (dd ^ d)
                    perm.append((src, dst))
        return lax.ppermute(a, ("mp", "dp"), perm)


def halves(a, flag, axis):
    h = a.shape[axis] // 2
    kept = lax.dynamic_slice_in_dim(a, flag * h, h, axis)
    sent = lax.dynamic_slice_in_dim(a, (1 - flag) * h, h, axis)
    return kept, sent


def joined(own, got, flag, axis):
    first = jnp.where(flag == 0, own, got)
    second = jnp.where(flag == 0, got, own)
    return jnp.concatenate([first, second], axis=axis)


def bit(value, b):
    return (value // b) % 2


def shards(grid, inputs, out_grads, weight, enc_in, dec_in, enc_out, dec_out):
    g = grid
    g.place()
    nx, ny = g.nx, g.ny
    tok, fb = inputs.shape
    cols = out_grads.shape[1]
    features = fb * g.mp
    hidden = cols * g.mp
    factor = step_size / features

    xsteps = [(dict(x=b), bit(g.x, b)) for b in g.xbits]
    zsteps = [(dict(z=b), bit(g.z, b)) for b in g.zbits]

    def scatter_rows(a, steps):
        for where, flag in steps:
            kept, sent = halves(a, flag, 0)
            a = kept + g.swap(sent.astype(bf16), **where).astype(f32)
        return a

    def gather_rows(a, steps):
        for where, flag in reversed(steps):
            a = joined(a, g.swap(a, **where), flag, 0)
        return a

    def editor(rows, enc, dec, width):
        wide = rows.astype(f32)
        squares = jnp.sum((wide * wide).reshape(tok, -1, 128), axis=1)
        message = jnp.concatenate([dot(rows, enc), squares], axis=1)
        message = scatter_rows(message, xsteps + zsteps)
        r = enc.shape[1]
        total = jnp.sum(message[:, r:], axis=1, keepdims=True)
        act = jax.nn.relu(message[:, :r] * lax.rsqrt(total / width + epsilon)).astype(bf16)
        act = gather_rows(act, xsteps + zsteps)
        return (wide + dot(act, dec)).astype(bf16)

    def sum_mp(a, transpose=False):
        a = scatter_rows(a, xsteps)
        for where, _ in zsteps:
            a = a + g.swap(a.astype(bf16), **where).astype(f32)
        a = (a * factor).astype(bf16)
        if not transpose:
            return gather_rows(a, xsteps)
        w = a.shape[1] // ny
        rows = []
        for s in range(ny):
            part = a[:, s * w : (s + 1) * w]
            pieces = []
            for t in range(nx):
                got = g.swap(part, x=t, d=2 * s) if s or t else part
                pieces.append(lax.optimization_barrier(got))
            for _, flag in xsteps:
                pieces = [joined(p, q, flag, 0) for p, q in zip(pieces[::2], pieces[1::2])]
            rows.append(pieces[0])
        return jnp.concatenate([p[:, k * w // 2 : (k + 1) * w // 2] for k in range(2) for p in rows], axis=1)

    weights = [weight, g.swap(weight, d=1)]

    tokens = [inputs] + [g.swap(inputs, d=2 * s) for s in range(1, ny)]

    edited_in = editor(inputs, enc_in, dec_in, features)
    edited_grad = editor(out_grads, enc_out, dec_out, hidden)

    blocks = [inputs]
    for b in reversed(g.zbits[1:]):
        flag = bit(g.z, b) ^ bit(g.d, b)
        pairs = []
        for part in blocks:
            got = g.swap(part, z=b)
            pairs.append((jnp.where(flag == 0, part, got), jnp.where(flag == 0, got, part)))
        blocks = [p for pair in pairs for p in pair]
    if len(g.zbits) > 2:
        assert len(blocks) == ny
    low = bit(g.z, 1) ^ bit(g.d, 1)

    def widen(part):
        for where, flag in reversed(xsteps):
            part = joined(part, g.swap(part, **where), flag, 1)
        n = len(xsteps)
        part = part.reshape((tok,) + (2,) * n + (fb,))
        return part.transpose((0,) + tuple(reversed(range(1, n + 1))) + (n + 1,)).reshape(tok, nx * fb)

    def both_rows(part):
        other = g.swap(part, z=1)
        a = widen(part)
        b = widen(other)
        return jnp.where(low == 0, a, b), jnp.where(low == 0, b, a)

    far = []
    for s in range(1, ny):
        part = g.swap(blocks[s], d=2 * s)
        rows = both_rows(part)
        part = sum(dot(r, w) for r, w in zip(rows, weights))
        far.append(g.swap(part.astype(bf16), d=2 * s).astype(f32))
    rows = both_rows(blocks[0])
    base = sum(dot(r, w) for r, w in zip(rows, weights))

    pair = jnp.concatenate([edited_in, g.swap(edited_in, d=1)], axis=0)
    kernel = jnp.concatenate([dot_t(t, pair) for t in tokens], axis=1)
    kernel = sum_mp(kernel, transpose=True)
    chunk = tok // 2
    parts = [edited_grad]
    for s in range(1, ny):
        for h in range(2):
            parts.append(g.swap(edited_grad[h * chunk : (h + 1) * chunk], d=2 * s))
    grads = [jnp.concatenate(parts, axis=0)]
    grads.append(g.swap(grads[0], d=1))
    parts = [g.swap(edited_in, d=2 * s) for s in range(1, ny)]
    others = jnp.concatenate(parts, axis=0)
    edits_all = jnp.concatenate([edited_in, others, pair[tok:], g.swap(others, d=1)], axis=0)
    base = base + sum(far)
    base = lax.optimization_barrier(base)
    w = ny * tok
    post_full = base - (dot(kernel[:, :w], grads[0]) + dot(kernel[:, w:], grads[1]))
    cotangent = (out_grads.astype(f32) * silu_slope(post_full)).astype(bf16)

    near = [
        lax.optimization_barrier(lax.dynamic_slice_in_dim(weights[1], (g.x ^ t) * fb, fb, 0)) for t in range(nx)
    ]

    def weight_rows(k, t):
        return near[t] if k else lax.dynamic_slice_in_dim(weights[0], (g.x ^ t) * fb, fb, 0)

    def kept_rows(cot):
        return [lax.optimization_barrier(dot_t(cot, weight_rows(k, 0))) for k in range(2)]

    def over_x(cot, kept):
        total = list(kept)
        for t in range(1, nx):
            sent = []
            for k in range(2):
                sent.append(dot_t(cot, weight_rows(k, t)).astype(bf16))
            got = g.swap(jnp.stack(sent), x=t)
            total = [total[k] + got[k].astype(f32) for k in range(2)]
        return total

    def over_z0(pair):
        flag = bit(g.z, 1) ^ bit(g.d, 1)
        kept = jnp.where(flag == 0, pair[0], pair[1])
        sent = jnp.where(flag == 0, pair[1], pair[0]).astype(bf16)
        return kept + g.swap(sent, z=1).astype(f32)

    others = {}
    for h in range(2):
        for s in range(1, ny):
            others[s, h] = g.swap(cotangent[h * chunk : (h + 1) * chunk], d=2 * s)
    back_kernel = jnp.concatenate([dot_t(cotangent, p) for p in grads], axis=1)
    back_kernel = sum_mp(back_kernel)
    correction = dot(back_kernel, edits_all)
    own = kept_rows(cotangent)
    for t in range(1, nx):
        for k in range(2):
            sent = dot_t(cotangent, weight_rows(k, t)).astype(bf16)
            own[k] = own[k] + g.swap(sent, x=t).astype(f32)
    own = over_z0(own)
    far_kept = {}
    for s in range(1, ny):
        far_kept[s] = kept_rows(jnp.concatenate([others[s, h] for h in range(2)], axis=0))
    out = []
    for h in range(2):
        blocks = [lax.optimization_barrier(own[h * chunk : (h + 1) * chunk])]
        for s in range(1, ny):
            pair = over_x(others[s, h], [lax.optimization_barrier(p[h * chunk : (h + 1) * chunk]) for p in far_kept[s]])
            part = over_z0(pair)
            blocks.append(g.swap(part.astype(bf16), d=2 * s).astype(f32))
        for b in g.zbits[1:]:
            flag = bit(g.z, b) ^ bit(g.d, b)
            kept = [jnp.where(flag == 0, p, q) for p, q in zip(blocks[::2], blocks[1::2])]
            sent = [jnp.where(flag == 0, q, p).astype(bf16) for p, q in zip(blocks[::2], blocks[1::2])]
            blocks = [p + g.swap(q, z=b).astype(f32) for p, q in zip(kept, sent)]
        out.append((blocks[0] - correction[h * chunk : (h + 1) * chunk]).astype(bf16))
    grad_in = jnp.concatenate(out, axis=0)
    return (post_full.astype(bf16), grad_in)


def solution(mesh):
    grid = Grid(mesh.shape["mp"], mesh.shape["dp"])

    def body(*args):
        return shards(grid, *args)

    in_specs = (
        P("dp", "mp"),
        P("dp", "mp"),
        P("dp", "mp"),
        P("mp", None),
        P(None, "mp"),
        P("mp", None),
        P(None, "mp"),
    )
    out_specs = (P("dp", "mp"), P("dp", "mp"))
    return jax.shard_map(body, mesh=mesh, in_specs=in_specs, out_specs=out_specs, check_vma=False)
```

```python
import jax
import jax.numpy as jnp
from jax import lax
from jax.sharding import PartitionSpec as P


epsilon = 1e-06
step_size = 0.25
bf16 = jnp.bfloat16
f32 = jnp.float32


def silu_slope(value):
    sig = jax.nn.sigmoid(value)
    return sig * (1.0 + value * (1.0 - sig))


def dot(a, b):
    return jnp.dot(a, b, preferred_element_type=f32)


def dot_t(a, b):
    return lax.dot_general(a, b, (((a.ndim - 1,), (1,)), ((), ())), preferred_element_type=f32)


class Grid:
    def __init__(self, mp, dp):
        self.mp, self.dp = mp, dp
        self.nz, self.nx, self.ny = dp, mp // dp, dp // 2
        self.xbits = [1 << b for b in range(self.nx.bit_length() - 1)]
        self.zbits = [1 << b for b in range(self.nz.bit_length() - 1)]

    def place(self):
        m, d = lax.axis_index("mp"), lax.axis_index("dp")
        self.z, self.x = m // self.nx, m % self.nx
        self.d = d

    def swap(self, a, z=0, x=0, d=0):
        perm = []
        for zz in range(self.nz):
            for xx in range(self.nx):
                for dd in range(self.dp):
                    src = (zz * self.nx + xx) * self.dp + dd
                    dst = ((zz ^ z) * self.nx + (xx ^ x)) * self.dp + (dd ^ d)
                    perm.append((src, dst))
        return lax.ppermute(a, ("mp", "dp"), perm)


def halves(a, flag, axis):
    h = a.shape[axis] // 2
    kept = lax.dynamic_slice_in_dim(a, flag * h, h, axis)
    sent = lax.dynamic_slice_in_dim(a, (1 - flag) * h, h, axis)
    return kept, sent


def joined(own, got, flag, axis):
    first = jnp.where(flag == 0, own, got)
    second = jnp.where(flag == 0, got, own)
    return jnp.concatenate([first, second], axis=axis)


def bit(value, b):
    return (value // b) % 2


def shards(grid, inputs, out_grads, weight, enc_in, dec_in, enc_out, dec_out):
    g = grid
    g.place()
    nx, ny = g.nx, g.ny
    tok, fb = inputs.shape
    cols = out_grads.shape[1]
    features = fb * g.mp
    hidden = cols * g.mp
    factor = step_size / features

    xsteps = [(dict(x=b), bit(g.x, b)) for b in g.xbits]
    zsteps = [(dict(z=b), bit(g.z, b)) for b in g.zbits]

    def scatter_rows(a, steps):
        for where, flag in steps:
            kept, sent = halves(a, flag, 0)
            a = kept + g.swap(sent.astype(bf16), **where).astype(f32)
        return a

    def gather_rows(a, steps):
        for where, flag in reversed(steps):
            a = joined(a, g.swap(a, **where), flag, 0)
        return a

    def editor(rows, enc, dec, width):
        wide = rows.astype(f32)
        squares = jnp.sum((wide * wide).reshape(tok, -1, 128), axis=1)
        message = jnp.concatenate([dot(rows, enc), squares], axis=1)
        message = scatter_rows(message, xsteps + zsteps)
        r = enc.shape[1]
        total = jnp.sum(message[:, r:], axis=1, keepdims=True)
        act = jax.nn.relu(message[:, :r] * lax.rsqrt(total / width + epsilon)).astype(bf16)
        act = gather_rows(act, xsteps + zsteps)
        return (wide + dot(act, dec)).astype(bf16)

    def sum_mp(a, transpose=False):
        a = scatter_rows(a, xsteps)
        for where, _ in zsteps:
            a = a + g.swap(a.astype(bf16), **where).astype(f32)
        a = (a * factor).astype(bf16)
        if not transpose:
            return gather_rows(a, xsteps)
        w = a.shape[1] // ny
        rows = []
        for s in range(ny):
            part = a[:, s * w : (s + 1) * w]
            pieces = []
            for t in range(nx):
                got = g.swap(part, x=t, d=2 * s) if s or t else part
                pieces.append(lax.optimization_barrier(got))
            for _, flag in xsteps:
                pieces = [joined(p, q, flag, 0) for p, q in zip(pieces[::2], pieces[1::2])]
            rows.append(pieces[0])
        return jnp.concatenate([p[:, k * w // 2 : (k + 1) * w // 2] for k in range(2) for p in rows], axis=1)

    weights = [weight, g.swap(weight, d=1)]

    tokens = [inputs] + [g.swap(inputs, d=2 * s) for s in range(1, ny)]

    edited_in = editor(inputs, enc_in, dec_in, features)
    edited_grad = editor(out_grads, enc_out, dec_out, hidden)

    near = [
        lax.optimization_barrier(lax.dynamic_slice_in_dim(weights[1], (g.x ^ t) * fb, fb, 0)) for t in range(nx)
    ]

    def weight_rows(k, t):
        return near[t] if k else lax.dynamic_slice_in_dim(weights[0], (g.x ^ t) * fb, fb, 0)

    blocks = [inputs]
    for b in reversed(g.zbits[1:]):
        flag = bit(g.z, b) ^ bit(g.d, b)
        pairs = []
        for part in blocks:
            got = g.swap(part, z=b)
            pairs.append((jnp.where(flag == 0, part, got), jnp.where(flag == 0, got, part)))
        blocks = [p for pair in pairs for p in pair]
    if len(g.zbits) > 2:
        assert len(blocks) == ny
    low = bit(g.z, 1) ^ bit(g.d, 1)

    def over_features(part):
        other = g.swap(part, z=1)
        a = [part] + [g.swap(part, x=t) for t in range(1, nx)]
        b = [other] + [g.swap(other, x=t) for t in range(1, nx)]
        total = 0.0
        for t in range(nx):
            total += dot(jnp.where(low == 0, a[t], b[t]), weight_rows(0, t))
            total += dot(jnp.where(low == 0, b[t], a[t]), weight_rows(1, t))
        return total

    far = []
    for s in range(1, ny):
        part = g.swap(blocks[s], d=2 * s)
        part = over_features(part)
        far.append(g.swap(part.astype(bf16), d=2 * s).astype(f32))
    base = over_features(blocks[0])

    pair = jnp.concatenate([edited_in, g.swap(edited_in, d=1)], axis=0)
    kernel = jnp.concatenate([dot_t(t, pair) for t in tokens], axis=1)
    kernel = sum_mp(kernel, transpose=True)
    chunk = tok // 2
    parts = [edited_grad]
    for s in range(1, ny):
        for h in range(2):
            parts.append(g.swap(edited_grad[h * chunk : (h + 1) * chunk], d=2 * s))
    grads = [jnp.concatenate(parts, axis=0)]
    grads.append(g.swap(grads[0], d=1))
    parts = [g.swap(edited_in, d=2 * s) for s in range(1, ny)]
    others = jnp.concatenate(parts, axis=0)
    edits_all = jnp.concatenate([edited_in, others, pair[tok:], g.swap(others, d=1)], axis=0)
    base = base + sum(far)
    base = lax.optimization_barrier(base)
    w = ny * tok
    post_full = base - (dot(kernel[:, :w], grads[0]) + dot(kernel[:, w:], grads[1]))
    cotangent = (out_grads.astype(f32) * silu_slope(post_full)).astype(bf16)

    def kept_rows(cot):
        return [lax.optimization_barrier(dot_t(cot, weight_rows(k, 0))) for k in range(2)]

    def over_x(cot, kept):
        total = list(kept)
        for t in range(1, nx):
            sent = []
            for k in range(2):
                sent.append(dot_t(cot, weight_rows(k, t)).astype(bf16))
            got = g.swap(jnp.stack(sent), x=t)
            total = [total[k] + got[k].astype(f32) for k in range(2)]
        return total

    def over_z0(pair):
        flag = bit(g.z, 1) ^ bit(g.d, 1)
        kept = jnp.where(flag == 0, pair[0], pair[1])
        sent = jnp.where(flag == 0, pair[1], pair[0]).astype(bf16)
        return kept + g.swap(sent, z=1).astype(f32)

    others = {}
    for h in range(2):
        for s in range(1, ny):
            others[s, h] = g.swap(cotangent[h * chunk : (h + 1) * chunk], d=2 * s)
    back_kernel = jnp.concatenate([dot_t(cotangent, p) for p in grads], axis=1)
    back_kernel = sum_mp(back_kernel)
    correction = dot(back_kernel, edits_all)
    own = kept_rows(cotangent)
    for t in range(1, nx):
        for k in range(2):
            sent = dot_t(cotangent, weight_rows(k, t)).astype(bf16)
            own[k] = own[k] + g.swap(sent, x=t).astype(f32)
    own = over_z0(own)
    far_kept = {}
    for s in range(1, ny):
        far_kept[s] = kept_rows(jnp.concatenate([others[s, h] for h in range(2)], axis=0))
    out = []
    for h in range(2):
        blocks = [lax.optimization_barrier(own[h * chunk : (h + 1) * chunk])]
        for s in range(1, ny):
            pair = over_x(others[s, h], [lax.optimization_barrier(p[h * chunk : (h + 1) * chunk]) for p in far_kept[s]])
            part = over_z0(pair)
            blocks.append(g.swap(part.astype(bf16), d=2 * s).astype(f32))
        for b in g.zbits[1:]:
            flag = bit(g.z, b) ^ bit(g.d, b)
            kept = [jnp.where(flag == 0, p, q) for p, q in zip(blocks[::2], blocks[1::2])]
            sent = [jnp.where(flag == 0, q, p).astype(bf16) for p, q in zip(blocks[::2], blocks[1::2])]
            blocks = [p + g.swap(q, z=b).astype(f32) for p, q in zip(kept, sent)]
        out.append((blocks[0] - correction[h * chunk : (h + 1) * chunk]).astype(bf16))
    grad_in = jnp.concatenate(out, axis=0)
    return (post_full.astype(bf16), grad_in)


def solution(mesh):
    grid = Grid(mesh.shape["mp"], mesh.shape["dp"])

    def body(*args):
        return shards(grid, *args)

    in_specs = (
        P("dp", "mp"),
        P("dp", "mp"),
        P("dp", "mp"),
        P("mp", None),
        P(None, "mp"),
        P("mp", None),
        P(None, "mp"),
    )
    out_specs = (P("dp", "mp"), P("dp", "mp"))
    return jax.shard_map(body, mesh=mesh, in_specs=in_specs, out_specs=out_specs, check_vma=False)
```

```python
import jax
import jax.numpy as jnp
from jax import lax
from jax.sharding import PartitionSpec as P


epsilon = 1e-06
step_size = 0.25
bf16 = jnp.bfloat16
f32 = jnp.float32


def silu_slope(value):
    sig = jax.nn.sigmoid(value)
    return sig * (1.0 + value * (1.0 - sig))


def dot(a, b):
    return jnp.dot(a, b, preferred_element_type=f32)


def dot_t(a, b):
    return lax.dot_general(a, b, (((a.ndim - 1,), (1,)), ((), ())), preferred_element_type=f32)


class Grid:
    def __init__(self, mp, dp):
        self.mp, self.dp = mp, dp
        self.nz, self.nx, self.ny = dp, mp // dp, dp // 2
        self.xbits = [1 << b for b in range(self.nx.bit_length() - 1)]
        self.zbits = [1 << b for b in range(self.nz.bit_length() - 1)]

    def place(self):
        m, d = lax.axis_index("mp"), lax.axis_index("dp")
        self.z, self.x = m // self.nx, m % self.nx
        self.d = d

    def swap(self, a, z=0, x=0, d=0):
        perm = []
        for zz in range(self.nz):
            for xx in range(self.nx):
                for dd in range(self.dp):
                    src = (zz * self.nx + xx) * self.dp + dd
                    dst = ((zz ^ z) * self.nx + (xx ^ x)) * self.dp + (dd ^ d)
                    perm.append((src, dst))
        return lax.ppermute(a, ("mp", "dp"), perm)


def halves(a, flag, axis):
    h = a.shape[axis] // 2
    kept = lax.dynamic_slice_in_dim(a, flag * h, h, axis)
    sent = lax.dynamic_slice_in_dim(a, (1 - flag) * h, h, axis)
    return kept, sent


def joined(own, got, flag, axis):
    first = jnp.where(flag == 0, own, got)
    second = jnp.where(flag == 0, got, own)
    return jnp.concatenate([first, second], axis=axis)


def bit(value, b):
    return (value // b) % 2


def shards(grid, inputs, out_grads, weight, enc_in, dec_in, enc_out, dec_out):
    g = grid
    g.place()
    nx, ny = g.nx, g.ny
    tok, fb = inputs.shape
    cols = out_grads.shape[1]
    features = fb * g.mp
    hidden = cols * g.mp
    factor = step_size / features

    xsteps = [(dict(x=b), bit(g.x, b)) for b in g.xbits]
    zsteps = [(dict(z=b), bit(g.z, b)) for b in g.zbits]

    def scatter_rows(a, steps):
        for where, flag in steps:
            kept, sent = halves(a, flag, 0)
            a = kept + g.swap(sent.astype(bf16), **where).astype(f32)
        return a

    def gather_rows(a, steps):
        for where, flag in reversed(steps):
            a = joined(a, g.swap(a, **where), flag, 0)
        return a

    def editor(rows, enc, dec, width):
        wide = rows.astype(f32)
        squares = jnp.sum((wide * wide).reshape(tok, -1, 128), axis=1)
        message = jnp.concatenate([dot(rows, enc), squares], axis=1)
        message = scatter_rows(message, xsteps + zsteps)
        r = enc.shape[1]
        total = jnp.sum(message[:, r:], axis=1, keepdims=True)
        act = jax.nn.relu(message[:, :r] * lax.rsqrt(total / width + epsilon)).astype(bf16)
        act = gather_rows(act, xsteps + zsteps)
        return (wide + dot(act, dec)).astype(bf16)

    def sum_mp(a, transpose=False):
        a = scatter_rows(a, xsteps)
        for where, _ in zsteps:
            a = a + g.swap(a.astype(bf16), **where).astype(f32)
        a = (a * factor).astype(bf16)
        if not transpose:
            return gather_rows(a, xsteps)
        w = a.shape[1] // ny
        rows = []
        for s in range(ny):
            part = a[:, s * w : (s + 1) * w]
            pieces = []
            for t in range(nx):
                got = g.swap(part, x=t, d=2 * s) if s or t else part
                pieces.append(lax.optimization_barrier(got))
            for _, flag in xsteps:
                pieces = [joined(p, q, flag, 0) for p, q in zip(pieces[::2], pieces[1::2])]
            rows.append(pieces[0])
        return jnp.concatenate([p[:, k * w // 2 : (k + 1) * w // 2] for k in range(2) for p in rows], axis=1)

    weights = [weight, g.swap(weight, d=1)]

    tokens = [inputs] + [g.swap(inputs, d=2 * s) for s in range(1, ny)]

    edited_in = editor(inputs, enc_in, dec_in, features)
    edited_grad = editor(out_grads, enc_out, dec_out, hidden)

    near = []
    for t in range(nx):
        near.append(lax.optimization_barrier(lax.dynamic_slice_in_dim(weights[1], (g.x ^ t) * fb, fb, 0)))

    def weight_rows(k, t):
        return near[t] if k else lax.dynamic_slice_in_dim(weights[0], (g.x ^ t) * fb, fb, 0)

    blocks = [inputs]
    for b in reversed(g.zbits[1:]):
        flag = bit(g.z, b) ^ bit(g.d, b)
        pairs = []
        for part in blocks:
            got = g.swap(part, z=b)
            pairs.append((jnp.where(flag == 0, part, got), jnp.where(flag == 0, got, part)))
        blocks = [p for pair in pairs for p in pair]
    if len(g.zbits) > 2:
        assert len(blocks) == ny
    low = bit(g.z, 1) ^ bit(g.d, 1)

    def over_features(part):
        other = g.swap(part, z=1)
        a = [part] + [g.swap(part, x=t) for t in range(1, nx)]
        b = [other] + [g.swap(other, x=t) for t in range(1, nx)]
        total = 0.0
        for t in range(nx):
            total += dot(jnp.where(low == 0, a[t], b[t]), weight_rows(0, t))
            total += dot(jnp.where(low == 0, b[t], a[t]), weight_rows(1, t))
        return total

    far = []
    for s in range(1, ny):
        part = g.swap(blocks[s], d=2 * s)
        part = over_features(part)
        far.append(g.swap(part.astype(bf16), d=2 * s).astype(f32))
    base = over_features(blocks[0])

    pair = jnp.concatenate([edited_in, g.swap(edited_in, d=1)], axis=0)
    kernel = jnp.concatenate([dot_t(t, pair) for t in tokens], axis=1)
    kernel = sum_mp(kernel, transpose=True)
    chunk = tok // 2
    parts = [edited_grad]
    for s in range(1, ny):
        for h in range(2):
            parts.append(g.swap(edited_grad[h * chunk : (h + 1) * chunk], d=2 * s))
    grads = [jnp.concatenate(parts, axis=0)]
    grads.append(g.swap(grads[0], d=1))
    parts = [g.swap(edited_in, d=2 * s) for s in range(1, ny)]
    others = jnp.concatenate(parts, axis=0)
    edits_all = jnp.concatenate([edited_in, others, pair[tok:], g.swap(others, d=1)], axis=0)
    base = base + sum(far)
    base = lax.optimization_barrier(base)
    w = ny * tok
    post_full = base - (dot(kernel[:, :w], grads[0]) + dot(kernel[:, w:], grads[1]))
    cotangent = (out_grads.astype(f32) * silu_slope(post_full)).astype(bf16)

    def kept_rows(cot):
        return [lax.optimization_barrier(dot_t(cot, weight_rows(k, 0))) for k in range(2)]

    def over_x(cot, kept):
        total = list(kept)
        for t in range(1, nx):
            sent = []
            for k in range(2):
                sent.append(dot_t(cot, weight_rows(k, t)).astype(bf16))
            got = g.swap(jnp.stack(sent), x=t)
            total = [total[k] + got[k].astype(f32) for k in range(2)]
        return total

    def over_z0(pair):
        flag = bit(g.z, 1) ^ bit(g.d, 1)
        kept = jnp.where(flag == 0, pair[0], pair[1])
        sent = jnp.where(flag == 0, pair[1], pair[0]).astype(bf16)
        return kept + g.swap(sent, z=1).astype(f32)

    others = {}
    for h in range(2):
        for s in range(1, ny):
            others[s, h] = g.swap(cotangent[h * chunk : (h + 1) * chunk], d=2 * s)
    back_kernel = jnp.concatenate([dot_t(cotangent, p) for p in grads], axis=1)
    back_kernel = sum_mp(back_kernel)
    correction = dot(back_kernel, edits_all)
    own = kept_rows(cotangent)
    for t in range(1, nx):
        for k in range(2):
            sent = dot_t(cotangent, weight_rows(k, t)).astype(bf16)
            own[k] = own[k] + g.swap(sent, x=t).astype(f32)
    own = over_z0(own)
    far_kept = {}
    for s in range(1, ny):
        far_kept[s] = kept_rows(jnp.concatenate([others[s, h] for h in range(2)], axis=0))
    out = []
    for h in range(2):
        blocks = [lax.optimization_barrier(own[h * chunk : (h + 1) * chunk])]
        for s in range(1, ny):
            pair = over_x(others[s, h], [lax.optimization_barrier(p[h * chunk : (h + 1) * chunk]) for p in far_kept[s]])
            part = over_z0(pair)
            blocks.append(g.swap(part.astype(bf16), d=2 * s).astype(f32))
        for b in g.zbits[1:]:
            flag = bit(g.z, b) ^ bit(g.d, b)
            kept = [jnp.where(flag == 0, p, q) for p, q in zip(blocks[::2], blocks[1::2])]
            sent = [jnp.where(flag == 0, q, p).astype(bf16) for p, q in zip(blocks[::2], blocks[1::2])]
            blocks = [p + g.swap(q, z=b).astype(f32) for p, q in zip(kept, sent)]
        out.append((blocks[0] - correction[h * chunk : (h + 1) * chunk]).astype(bf16))
    grad_in = lax.optimization_barrier(jnp.concatenate([out[0], out[0]], axis=0))
    grad_in = lax.dynamic_update_slice(grad_in, out[1], (chunk, 0))
    return (post_full.astype(bf16), grad_in)


def solution(mesh):
    grid = Grid(mesh.shape["mp"], mesh.shape["dp"])

    def body(*args):
        return shards(grid, *args)

    in_specs = (
        P("dp", "mp"),
        P("dp", "mp"),
        P("dp", "mp"),
        P("mp", None),
        P(None, "mp"),
        P("mp", None),
        P(None, "mp"),
    )
    out_specs = (P("dp", "mp"), P("dp", "mp"))
    return jax.shard_map(body, mesh=mesh, in_specs=in_specs, out_specs=out_specs, check_vma=False)
```
